32 devices in a mesh: clip: 2 (over y), frames: 4 (over z), rows: 2 (over x), heads: 2 (over core).
Axes of the slice: x: 2, y: 2, z: 4, core: 2. Of those that a mesh axis runs over, the one named last changes fastest.
Arguments:
- tok_q: bfloat16 [64, 32, 1536], P(('clip', 'frames'), 'rows', 'heads'), parts along dimension 0, may hold values from -125 to 125, as said below
- tok_kv: bfloat16 [2, 64, 32, 1536], P(None, ('clip', 'frames'), 'rows', 'heads'), parts along dimension 1, may hold values from -6 to 6
- ref_kv: bfloat16 [2, 4, 768, 1536], P(None, 'clip', ('frames', 'rows'), 'heads'), parts along dimension 1, may hold values from -6 to 6
- ref_ids: int32 [64], P(('clip', 'frames')), parts along dimension 0, may hold values from 0 to 1
Outputs:
- mixed: bfloat16 [64, 32, 1536], P(('clip', 'frames'), 'rows', 'heads'), parts along dimension 0
The draws below stay inside these ranges and needn't reach their ends.
There are 2 independent parts, one for each index of `clip`. The reference program is written for one: setup_inputs(seed, part) draws one part's arguments, and reference() takes and returns one part's arrays. A program takes and returns all parts, laid end to end along the dimension named above; each array names one. Nothing has to cross between parts.
Inputs may be any that keep to these rules, and one draw needn't show every extreme that they name: `tok_q`: queries of the clip's tokens.
All inputs are finite; a program needn't handle non-finite values.
Results may differ from the reference program's by a relative error of at most 0.0048.
Values may be sent and summed in bfloat16 or wider, within the bound.
No kernel may reach another device: no remote copies, remote signals or barrier semaphores. Data moves between devices by JAX's collectives and lax.ppermute only.
A program may use at most 64 MiB of HBM per device.

```python
import jax
import jax.numpy as jnp
from jax import lax

HEADS = 12
HEAD_DIM = 128
BAND = 8
NREF = 2
REF_TOK = 768
WIDTH = 1536
FRAMES = 32
TOK = 32


def token_fields(key):
    base = jax.random.fold_in(key, 11)
    seed_query, seed_keys, seed_values = jax.random.split(base, 3)
    shape = (FRAMES, TOK, HEADS * HEAD_DIM)
    query = 2.0 * jnp.clip(jax.random.normal(seed_query, shape, jnp.float32), -6.0, 6.0)
    keys_raw = jnp.clip(jax.random.normal(seed_keys, shape, jnp.float32), -5.0, 5.0)
    values = jnp.clip(jax.random.normal(seed_values, shape, jnp.float32), -6.0, 6.0)
    return (query, jnp.stack([keys_raw, values]))


def draw_tok_q(key, part):
    return token_fields(key)[0].astype(jnp.bfloat16)


def draw_tok_kv(key, part):
    return token_fields(key)[1].astype(jnp.bfloat16)


def set_ends(result, key, least, high):
    longest = result.shape.index(max(result.shape))
    spots = []
    for shift in (0, 1):
        where = [jax.random.randint(jax.random.fold_in(key, axis), (), 0, length) for axis, length in enumerate(result.shape)]
        where[longest] = (where[longest] + shift) % result.shape[longest]
        spots.append(tuple(where))
    return result.at[spots[0]].set(least).at[spots[1]].set(high)


def shard_levels(stream_key, dims, shards, low, high):
    level, own = 1.0, jax.random.fold_in(stream_key, 6)
    for dim, shards_of in shards:
        draws = jnp.exp(jax.random.uniform(jax.random.fold_in(own, dim), (shards_of,), jnp.float32, low / len(shards), high / len(shards)))
        level = level * jnp.repeat(draws, dims[dim] // shards_of).reshape([-1 if axis == dim else 1 for axis in range(len(dims))])
    return level


def normal_values(rng, extent, scale, bound, cuts=(), held_as=jnp.bfloat16):
    loudness = shard_levels(rng, extent, cuts, -0.22, 0.18) if cuts else 1.0
    drawn = jax.random.normal(rng, extent, jnp.float32) * scale * loudness
    return jnp.minimum(jnp.maximum(drawn, -bound), bound).astype(held_as)


def setup_inputs(seed: int = 0, part: int = 0) -> dict:
    key_of = jax.random.split(jax.random.key(seed), 5)
    own_keys = jax.random.split(jax.random.fold_in(key_of[4], part), 5)
    return {
        "tok_q": draw_tok_q(jax.random.fold_in(jax.random.fold_in(key_of[4], part), 71), part),
        "tok_kv": draw_tok_kv(jax.random.fold_in(jax.random.fold_in(key_of[4], part), 71), part),
        "ref_kv": normal_values(own_keys[2], (2, NREF, REF_TOK, WIDTH), 1.0, 6.0, ((2, 8), (3, 2))),
        "ref_ids": set_ends(jax.random.randint(own_keys[3], (FRAMES,), 0, NREF), jax.random.fold_in(own_keys[3], 1), 0, NREF - 1).astype(jnp.int32),
    }


def reference(tok_q, tok_kv, ref_kv, ref_ids):
    frame_total = tok_q.shape[0]
    factor = 1.0 / (HEAD_DIM ** 0.5)
    offsets = jnp.arange(-BAND, BAND + 1, dtype=jnp.int32)

    def one_frame(frame):
        query = tok_q[frame].astype(jnp.float32).reshape(TOK, HEADS, HEAD_DIM)
        window = ((frame + offsets) % frame_total).astype(jnp.int32)
        band_keys = jnp.take(tok_kv[0], window, axis=0).astype(jnp.float32).reshape(2 * BAND + 1, TOK, HEADS, HEAD_DIM)
        band_values = jnp.take(tok_kv[1], window, axis=0).astype(jnp.float32).reshape(2 * BAND + 1, TOK, HEADS, HEAD_DIM)
        band_scores = jnp.einsum('thd,othd->oth', query, band_keys) * factor
        band_weights = lax.optimization_barrier(jax.nn.softmax(band_scores, axis=0).astype(jnp.bfloat16)).astype(jnp.float32)
        temporal = jnp.einsum('oth,othd->thd', band_weights, band_values)
        frame_keys = tok_kv[0, frame].astype(jnp.float32).reshape(TOK, HEADS, HEAD_DIM)
        frame_values = tok_kv[1, frame].astype(jnp.float32).reshape(TOK, HEADS, HEAD_DIM)
        chosen = jnp.take(ref_kv, ref_ids[frame], axis=1)
        image_keys = chosen[0].astype(jnp.float32).reshape(REF_TOK, HEADS, HEAD_DIM)
        image_values = chosen[1].astype(jnp.float32).reshape(REF_TOK, HEADS, HEAD_DIM)
        local_scores = jnp.einsum('thd,shd->hts', query, frame_keys) * factor
        image_scores = jnp.einsum('thd,shd->hts', query, image_keys) * factor
        top = jnp.maximum(jnp.max(local_scores, axis=-1), jnp.max(image_scores, axis=-1))
        local_exp = jnp.exp(local_scores - top[..., None])
        image_exp = jnp.exp(image_scores - top[..., None])
        total = jnp.sum(local_exp, axis=-1) + jnp.sum(image_exp, axis=-1)
        local_weights = lax.optimization_barrier((local_exp / total[..., None]).astype(jnp.bfloat16)).astype(jnp.float32)
        image_weights = lax.optimization_barrier((image_exp / total[..., None]).astype(jnp.bfloat16)).astype(jnp.float32)
        spatial = jnp.einsum('hts,shd->thd', local_weights, frame_values) + jnp.einsum('hts,shd->thd', image_weights, image_values)
        return (temporal + spatial).reshape(TOK, HEADS * HEAD_DIM).astype(jnp.bfloat16)

    return lax.map(one_frame, jnp.arange(frame_total, dtype=jnp.int32))
```

```python
import functools

import jax
import jax.numpy as jnp
from jax import lax
from jax.experimental import pallas as pl
from jax.experimental.pallas import tpu as pltpu
from jax.sharding import PartitionSpec as P

HEAD_DIM = 128
BAND = 8
LANES = 128
SUB = 8
TILE = 16
NEG = -1e30


def round_up(value, step):
    return -(-value // step) * step


def shifted(value, axis, shift):
    devices = lax.axis_size(axis)
    return lax.ppermute(value, axis, [(i, (i + shift) % devices) for i in range(devices)])


def call(body, outs, *args, smem=()):
    vmem = pl.BlockSpec(memory_space=pltpu.VMEM)
    specs = [pl.BlockSpec(memory_space=pltpu.SMEM) if i in smem else vmem for i in range(len(args))]
    return pl.pallas_call(
        body,
        out_shape=outs,
        in_specs=specs,
        out_specs=jax.tree.map(lambda _: vmem, outs),
    )(*args)


def scores_of(query, keys, factor):
    return (
        lax.dot_general(query, keys, (((1,), (1,)), ((), ())), preferred_element_type=jnp.float32)
        * factor
    )


def weighted(weights, values):
    return jnp.dot(weights.astype(jnp.bfloat16), values, preferred_element_type=jnp.float32)


def softmax_parts(parts):
    top = functools.reduce(jnp.maximum, [jnp.max(s, axis=1, keepdims=True) for s in parts])
    exps = [jnp.exp(s - top) for s in parts]
    total = functools.reduce(jnp.add, [jnp.sum(e, axis=1, keepdims=True) for e in exps])
    return exps, total, top + jnp.log(total)


def frame_rows(pieces, rows):
    return jnp.concatenate([jnp.broadcast_to(p, (rows, LANES)) for p in pieces], axis=0)


def band_mask(frames, rows, offset):
    count = frames * rows
    row = lax.broadcasted_iota(jnp.int32, (count, count), 0)
    col = lax.broadcasted_iota(jnp.int32, (count, count), 1)
    gap = col // rows + offset - row // rows
    return (col % rows == row % rows) & (jnp.abs(gap) <= BAND)


def frame_mask(frames, rows):
    count = frames * rows
    row = lax.broadcasted_iota(jnp.int32, (count, count), 0)
    col = lax.broadcasted_iota(jnp.int32, (count, count), 1)
    return col // rows == row // rows


def head_of(ref, index, h):
    block = ref[index, :, :, h * HEAD_DIM : (h + 1) * HEAD_DIM]
    return block.reshape(block.shape[0] * block.shape[1], HEAD_DIM)


def to_rows(columns, nq):
    lane = lax.broadcasted_iota(jnp.int32, (nq, LANES), 1)
    held = jnp.zeros((nq, LANES), jnp.float32)
    for i, column in enumerate(columns):
        held = jnp.where(lane == i, column, held)
    return held.T[: round_up(len(columns), SUB)]


def split_rows(rows):
    first = rows.astype(jnp.bfloat16).astype(jnp.float32)
    rest = rows - first
    second = rest.astype(jnp.bfloat16).astype(jnp.float32)
    pieces = jnp.concatenate([first, second, rest - second], axis=0)
    pad = round_up(pieces.shape[0], TILE) - pieces.shape[0]
    if pad:
        pieces = jnp.concatenate([pieces, jnp.zeros((pad, pieces.shape[1]), jnp.float32)], axis=0)
    return pieces.astype(jnp.bfloat16)


def joined_rows(pieces, count):
    pieces = pieces.astype(jnp.float32)
    return (pieces[:count] + pieces[count : 2 * count]) + pieces[2 * count : 3 * count]


def spread(which, width):
    return which[:, :width] if width <= LANES else which[:, :1]


def spatial_scores(query, refs, images, h, which, valid, factor):
    lanes = slice(h * HEAD_DIM, (h + 1) * HEAD_DIM)
    parts = []
    for ref in refs:
        score = scores_of(query, ref[0, 0, :, lanes], factor)
        for i in range(1, images):
            other = scores_of(query, ref[0, i, :, lanes], factor)
            score = jnp.where(spread(which, score.shape[1]) == i, other, score)
        if valid < score.shape[1]:
            col = lax.broadcasted_iota(jnp.int32, score.shape, 1)
            score = jnp.where(col < valid, score, NEG)
        parts.append(score)
    return parts


def spatial_values(exps, refs, images, h, which):
    lanes = slice(h * HEAD_DIM, (h + 1) * HEAD_DIM)
    total = None
    for e, ref in zip(exps, refs):
        for i in range(images):
            mine = jnp.where(spread(which, e.shape[1]) == i, e, 0.0)
            term = weighted(mine, ref[1, i, :, lanes])
            total = term if total is None else total + term
    return total


def pack_body(frames, heads, ids_ref, query_ref, out_ref):
    nq = query_ref.shape[0] * query_ref.shape[1]
    for h in range(heads):
        block = query_ref[:, :, h * HEAD_DIM : (h + 1) * HEAD_DIM]
        out_ref[h * nq : (h + 1) * nq, :] = block.reshape(nq, HEAD_DIM)
    pad = out_ref.shape[0] - heads * nq
    row = lax.broadcasted_iota(jnp.int32, (pad, LANES), 0)
    held = jnp.zeros((pad, LANES), jnp.float32)
    for f in range(frames):
        held = jnp.where(row == f, ids_ref[f].astype(jnp.float32), held)
    out_ref[heads * nq :, :] = held.astype(jnp.bfloat16)


def temporal_body(frames, rows, heads, offsets, factor, *refs):
    nq = frames * rows
    count = len(offsets)
    queries, kv, outs = refs[:count], refs[count], refs[count + 1 :]
    for query_ref, offset, out in zip(queries, offsets, outs):
        mask = band_mask(frames, rows, offset)
        logs = []
        for h in range(heads):
            query = query_ref[h * nq : (h + 1) * nq, :]
            score = scores_of(query, head_of(kv, 0, h), factor)
            (e,), total, log = softmax_parts([jnp.where(mask, score, NEG)])
            out[h * nq : (h + 1) * nq, :] = (weighted(e, head_of(kv, 1, h)) / total).astype(out.dtype)
            logs.append(log)
        out[heads * nq :, :] = split_rows(to_rows(logs, nq))


def spatial_body(frames, rows, heads, parts, images, valid, factor, query_ref, *refs):
    nq = frames * rows
    sources, out = refs[:parts], refs[parts]
    held = query_ref[heads * nq :, :].astype(jnp.float32)
    which = frame_rows([held[f : f + 1] for f in range(frames)], rows)
    logs = []
    for h in range(heads):
        query = query_ref[h * nq : (h + 1) * nq, :]
        exps, total, log = softmax_parts(
            spatial_scores(query, sources, images, h, which, valid, factor)
        )
        result = spatial_values(exps, sources, images, h, which) / total
        out[h * nq : (h + 1) * nq, :] = result.astype(out.dtype)
        logs.append(log)
    out[heads * nq :, :] = split_rows(to_rows(logs, nq))


def own_body(frames, rows, heads, parts, images, valid, sides, offsets, factor, ids_ref, query_ref, *refs):
    nq = frames * rows
    sources, refs = refs[:parts], refs[parts:]
    others, refs = refs[:sides], refs[sides:]
    blocks, refs = refs[: len(offsets)], refs[len(offsets) :]
    out_s, out_t, out_l = refs
    which = frame_rows([ids_ref[f].astype(jnp.float32) for f in range(frames)], rows)
    same = frame_mask(frames, rows)
    bands = [band_mask(frames, rows, offset) for offset in offsets]
    logs_s, logs_t = [], []
    for h in range(heads):
        query = query_ref[:, :, h * HEAD_DIM : (h + 1) * HEAD_DIM].reshape(nq, HEAD_DIM)
        near = [
            jnp.where(same, scores_of(query, head_of(kv, 0, h), factor), NEG) for kv in others
        ]
        far = spatial_scores(query, sources, images, h, which, valid, factor)
        exps, total, log = softmax_parts(near + far)
        result = spatial_values(exps[sides:], sources, images, h, which)
        for e, kv in zip(exps, others):
            result = result + weighted(e, head_of(kv, 1, h))
        out_s[h * nq : (h + 1) * nq, :] = result / total
        logs_s.append(log)
        scores = [
            jnp.where(band, scores_of(query, head_of(kv, 0, h), factor), NEG)
            for kv, band in zip(blocks, bands)
        ]
        exps, total, log = softmax_parts(scores)
        result = functools.reduce(
            jnp.add, [weighted(e, head_of(kv, 1, h)) for e, kv in zip(exps, blocks)]
        )
        out_t[h * nq : (h + 1) * nq, :] = result / total
        logs_t.append(log)
    count = round_up(heads, SUB)
    out_l[:count, :] = to_rows(logs_s, nq)
    out_l[count:, :] = to_rows(logs_t, nq)


def final_body(heads, spatial, temporal, *refs):
    own_s, own_t, own_l = refs[:3]
    messages = refs[3 : 3 + spatial + temporal]
    out = refs[-1]
    nq = own_s.shape[0] // heads
    count = round_up(heads, SUB)
    logs = [joined_rows(m[heads * nq :, :], count) for m in messages]
    weights = []
    for own, others in (
        (own_l[:count, :], logs[:spatial]),
        (own_l[count:, :], logs[spatial:]),
    ):
        top = functools.reduce(jnp.maximum, [own, *others])
        exps = [jnp.exp(log - top) for log in [own, *others]]
        total = functools.reduce(jnp.add, exps)
        weights += [e / total for e in exps]
    stacked = jnp.concatenate(weights, axis=0)
    pad = LANES - stacked.shape[0]
    columns = jnp.concatenate([stacked, jnp.zeros((pad, nq), jnp.float32)], axis=0).T
    values = [own_s, *messages[:spatial], own_t, *messages[spatial:]]
    for h in range(heads):
        total = None
        for i, value in enumerate(values):
            at = i * count + h
            term = columns[:, at : at + 1] * value[h * nq : (h + 1) * nq, :].astype(jnp.float32)
            total = term if total is None else total + term
        block = total.astype(out.dtype).reshape(out.shape[0], out.shape[1], HEAD_DIM)
        out[:, :, h * HEAD_DIM : (h + 1) * HEAD_DIM] = block


def padded_tokens(ref_kv):
    pad = round_up(ref_kv.shape[2], TILE) - ref_kv.shape[2]
    return jnp.pad(ref_kv, ((0, 0), (0, 0), (0, pad), (0, 0))) if pad else ref_kv


def local(tok_q, tok_kv, ref_kv, ref_ids):
    frames, rows, width = tok_q.shape
    heads, nq = width // HEAD_DIM, frames * rows
    images, factor = ref_kv.shape[1], 1.0 / HEAD_DIM**0.5
    along, across = lax.axis_size("frames"), lax.axis_size("rows")
    reach = (BAND - 1) // frames + 1
    assert 2 * reach + 1 <= along and nq == LANES and frames <= TILE
    near = [s for r in range(1, reach + 1) for s in (r, along - r)]
    signed = {s: s if s <= reach else s - along for s in near}
    side_kv = [shifted(tok_kv, "rows", s) for s in range(1, across)]
    travel = 2 * tok_q.size < across * ref_kv.size
    f32, bf16 = jnp.float32, jnp.bfloat16
    own_shape = (
        jax.ShapeDtypeStruct((heads * nq, HEAD_DIM), f32),
        jax.ShapeDtypeStruct((heads * nq, HEAD_DIM), f32),
        jax.ShapeDtypeStruct((2 * round_up(heads, SUB), nq), f32),
    )
    if travel:
        ref = padded_tokens(ref_kv)
        valid = ref_kv.shape[2]
        packed = call(
            functools.partial(pack_body, frames, heads),
            jax.ShapeDtypeStruct((heads * nq + TILE, HEAD_DIM), bf16),
            ref_ids,
            tok_q,
            smem=(0,),
        )
        shifts = near + [s for s in range(1, along) if s not in near]
        queries = {s: shifted(packed, "frames", s) for s in shifts}
        refs = [ref] + [shifted(ref, "rows", s) for s in range(1, across)]
        message = jax.ShapeDtypeStruct(
            (heads * nq + round_up(3 * round_up(heads, SUB), TILE), HEAD_DIM), bf16
        )
        partial_t = call(
            functools.partial(
                temporal_body, frames, rows, heads, [signed[s] * frames for s in near], factor
            ),
            [message] * len(near),
            *[queries[s] for s in near],
            tok_kv,
        )
        back_t = [shifted(m, "frames", along - s) for m, s in zip(partial_t, near)]
        back_s = []
        for s in shifts:
            partial_s = call(
                functools.partial(
                    spatial_body, frames, rows, heads, len(refs), images, valid, factor
                ),
                message,
                queries[s],
                *refs,
            )
            back_s.append(shifted(partial_s, "frames", along - s))
        blocks, offsets = [tok_kv], [0]
    else:
        gathered = lax.all_gather(ref_kv, ("frames", "rows"), axis=2, tiled=True)
        valid = gathered.shape[2]
        refs = [padded_tokens(gathered)]
        blocks = [tok_kv] + [shifted(tok_kv, "frames", s) for s in near]
        offsets = [0] + [-signed[s] * frames for s in near]
        back_s, back_t = [], []
    own = call(
        functools.partial(
            own_body, frames, rows, heads, len(refs), images, valid, across, offsets, factor
        ),
        own_shape,
        ref_ids,
        tok_q,
        *refs,
        tok_kv,
        *side_kv,
        *blocks,
        smem=(0,),
    )
    return call(
        functools.partial(final_body, heads, len(back_s), len(back_t)),
        jax.ShapeDtypeStruct(tok_q.shape, bf16),
        *own,
        *back_s,
        *back_t,
    )


def solution(mesh):
    placed = (
        P(("clip", "frames"), "rows", "heads"),
        P(None, ("clip", "frames"), "rows", "heads"),
        P(None, "clip", ("frames", "rows"), "heads"),
        P(("clip", "frames")),
    )
    return jax.shard_map(
        local,
        mesh=mesh,
        in_specs=placed,
        out_specs=P(("clip", "frames"), "rows", "heads"),
        check_vma=False,
    )
```

```python
import functools

import jax
import jax.numpy as jnp
from jax import lax
from jax.experimental import pallas as pl
from jax.experimental.pallas import tpu as pltpu
from jax.sharding import PartitionSpec as P

HEAD_DIM = 128
BAND = 8
LANES = 128
TILE = 16
NEG = -1e30
LOG2E = 1.4426950408889634
LN2 = 0.6931471805599453


def round_up(value, step):
    return -(-value // step) * step


class Call:
    def __init__(self, pinned):
        self.pinned = pinned

    def __call__(self, body, outs, *args, scalars=0, last=False):
        vmem, smem = pltpu.VMEM, pltpu.SMEM
        specs = [pl.BlockSpec(memory_space=smem if i < scalars else vmem) for i in range(len(args))]
        if self.pinned:
            args = [
                a if i < scalars else pltpu.with_memory_space_constraint(a, vmem)
                for i, a in enumerate(args)
            ]
        if self.pinned and not last:
            shapes = tuple(vmem(shape, dtype) for shape, dtype in outs)
        else:
            shapes = tuple(jax.ShapeDtypeStruct(shape, dtype) for shape, dtype in outs)
        return pl.pallas_call(
            body,
            out_shape=shapes,
            in_specs=specs,
            out_specs=tuple(pl.BlockSpec(memory_space=vmem) for _ in outs),
            compiler_params=pltpu.CompilerParams(
                vmem_limit_bytes=(24 if self.pinned else 48) * 2**20
            ),
        )(*args)


def times_transposed(left, right):
    return lax.dot_general(
        left, right, (((1,), (1,)), ((), ())), preferred_element_type=jnp.float32
    )


def transposed_times(left, right):
    return lax.dot_general(
        left, right, (((0,), (0,)), ((), ())), preferred_element_type=jnp.float32
    )


def softmax_parts(parts, factor):
    top = functools.reduce(jnp.maximum, [jnp.max(s, axis=0, keepdims=True) for s in parts])
    exps = [jnp.exp2((s - top) * (factor * LOG2E)) for s in parts]
    total = functools.reduce(jnp.add, [jnp.sum(e, axis=0, keepdims=True) for e in exps])
    return exps, total, top * factor + jnp.log(total)


def iotas(keys, queries):
    return (
        lax.broadcasted_iota(jnp.int32, (keys, queries), 0),
        lax.broadcasted_iota(jnp.int32, (keys, queries), 1),
    )


def band_mask(nq, rows, offset):
    key, query = iotas(nq, nq)
    gap = key // rows - query // rows + offset
    return (key % rows == query % rows) & (jnp.abs(gap) <= BAND)


def split_rows(rows):
    pieces = []
    for row in rows:
        first = row.astype(jnp.bfloat16).astype(jnp.float32)
        rest = row - first
        second = rest.astype(jnp.bfloat16).astype(jnp.float32)
        pieces += [first, second, rest - second]
    size = (round_up(len(pieces), TILE), rows[0].shape[1])
    at = lax.broadcasted_iota(jnp.int32, size, 0)
    held = jnp.zeros(size, jnp.float32)
    for i, piece in enumerate(pieces):
        held = jnp.where(at == i, piece, held)
    return held.astype(jnp.bfloat16)


def joined_rows(pieces, count):
    pieces = pieces.astype(jnp.float32)
    return [
        (pieces[3 * i : 3 * i + 1] + pieces[3 * i + 1 : 3 * i + 2]) + pieces[3 * i + 2 : 3 * i + 3]
        for i in range(count)
    ]


class Rows:
    def __init__(self, group, nq, images, tokens):
        self.group, self.nq, self.images, self.tokens = group, nq, images, tokens
        self.query = group * nq + TILE
        self.kv = 2 * group * nq
        self.ref = 2 * images * group * tokens
        self.all = self.query + self.kv + self.ref
        self.logs = round_up(3 * group, TILE)
        self.message = group * HEAD_DIM + self.logs

    def head(self, h):
        return slice(h * self.nq, (h + 1) * self.nq)

    def out(self, h, start=0):
        return slice(start + h * HEAD_DIM, start + (h + 1) * HEAD_DIM)

    def query_at(self, ref, h, start=0):
        return ref[start + h * self.nq : start + (h + 1) * self.nq, :]

    def which_at(self, ref, start=0):
        at = start + self.group * self.nq
        return ref[at : at + TILE, :].astype(jnp.float32)[:1]

    def kv_at(self, ref, i, h, start=0):
        at = start + (i * self.group + h) * self.nq
        return ref[at : at + self.nq, :]

    def ref_at(self, ref, i, image, h, start=0):
        at = start + ((i * self.images + image) * self.group + h) * self.tokens
        return ref[at : at + self.tokens, :]


def pack_body(lay, across, rows, place_ref, ids_ref, q_ref, kv_ref, ref_ref, *outs):
    nq, group, tokens = lay.nq, lay.group, lay.tokens
    lane = lax.broadcasted_iota(jnp.int32, (TILE, LANES), 1)
    held = jnp.zeros((TILE, LANES), jnp.float32)
    for f in range(ids_ref.shape[0]):
        held = jnp.where(lane // rows == f, ids_ref[f].astype(jnp.float32), held)
    which = held.astype(jnp.bfloat16)
    for r in range(across):
        first = lax.rem(place_ref[0] + r, across) * group
        out_q, out_kv, out_ref = outs[3 * r : 3 * r + 3]
        every = outs[3 * across + r - 1] if r else None

        def put(target, start, at, value):
            target[at : at + value.shape[0], :] = value
            if every is not None:
                every[start + at : start + at + value.shape[0], :] = value

        for h in range(group):
            lanes = pl.ds(pl.multiple_of((first + h) * HEAD_DIM, HEAD_DIM), HEAD_DIM)
            put(out_q, 0, h * nq, q_ref[:, :, lanes].reshape(nq, HEAD_DIM))
            for i in range(2):
                value = kv_ref[i, :, :, lanes].reshape(nq, HEAD_DIM)
                put(out_kv, lay.query, (i * group + h) * nq, value)
                for image in range(lay.images):
                    at = ((i * lay.images + image) * group + h) * tokens
                    put(out_ref, lay.query + lay.kv, at, ref_ref[i, image, :, lanes])
        put(out_q, 0, group * nq, which)


def spatial_scores(lay, query, which, sources, h):
    parts = []
    for ref, start in sources:
        score = times_transposed(lay.ref_at(ref, 0, 0, h, start), query)
        for image in range(1, lay.images):
            other = times_transposed(lay.ref_at(ref, 0, image, h, start), query)
            score = jnp.where(which == image, other, score)
        parts.append(score)
    return parts


def spatial_values(lay, exps, which, sources, h):
    total = None
    for e, (ref, start) in zip(exps, sources):
        for image in range(lay.images):
            mine = jnp.where(which == image, e, 0.0).astype(jnp.bfloat16)
            term = transposed_times(lay.ref_at(ref, 1, image, h, start), mine)
            total = term if total is None else total + term
    return total


def temporal_part(lay, query, blocks, masks, h, factor):
    parts = [
        jnp.where(mask, times_transposed(lay.kv_at(ref, 0, h, start), query), NEG)
        for (ref, start), mask in zip(blocks, masks)
    ]
    exps, total, log = softmax_parts(parts, factor)
    terms = [
        transposed_times(lay.kv_at(ref, 1, h, start), e.astype(jnp.bfloat16))
        for e, (ref, start) in zip(exps, blocks)
    ]
    return functools.reduce(jnp.add, terms) / total, log


def mirror_temporal_body(lay, rows, across, starts, factor, place_ref, *refs):
    queries, blocks, outs = refs[:across], refs[across : 2 * across], refs[2 * across :]
    mask = band_mask(lay.nq, rows, place_ref[1])
    for r in range(across):
        logs = []
        for h in range(lay.group):
            result, log = temporal_part(
                lay, lay.query_at(queries[r], h), [(blocks[r], starts[r])], [mask], h, factor
            )
            outs[r][lay.out(h), :] = result.astype(jnp.bfloat16)
            logs.append(log)
        outs[r][lay.group * HEAD_DIM :, :] = split_rows(logs)


def mirror_spatial_body(lay, across, starts, factor, *refs):
    queries, sources, outs = refs[:across], refs[across : across + len(starts)], refs[-across:]
    sources = list(zip(sources, starts))
    which = jnp.concatenate([lay.which_at(q) for q in queries], axis=1)
    logs = []
    for h in range(lay.group):
        query = jnp.concatenate([lay.query_at(q, h) for q in queries], axis=0)
        exps, total, log = softmax_parts(spatial_scores(lay, query, which, sources, h), factor)
        result = spatial_values(lay, exps, which, sources, h) / total
        for r, out in enumerate(outs):
            out[lay.out(h), :] = result[:, r * lay.nq : (r + 1) * lay.nq].astype(jnp.bfloat16)
        logs.append(log)
    for r, out in enumerate(outs):
        out[lay.group * HEAD_DIM :, :] = split_rows([g[:, r * lay.nq : (r + 1) * lay.nq] for g in logs])


def own_body(lay, rows, counts, starts, factor, place_ref, *refs):
    nquery, nsource, nnear, nfar = counts
    refs = list(zip(refs[: len(starts)], starts)) + list(refs[len(starts) :])
    queries, refs = refs[:nquery], refs[nquery:]
    sources, refs = refs[:nsource], refs[nsource:]
    near, refs = refs[:nnear], refs[nnear:]
    far = [refs[r * nfar : (r + 1) * nfar] for r in range(nquery)]
    out_s, out_t, out_l, *others = refs[nquery * nfar :]
    masks = [band_mask(lay.nq, rows, place_ref[2 + i]) for i in range(nfar)]
    key, query = iotas(lay.nq, nquery * lay.nq)
    same = key // rows == (query % lay.nq) // rows
    which = jnp.concatenate([lay.which_at(*q) for q in queries], axis=1)
    spatial_logs, temporal_logs = [], [[] for _ in queries]
    for h in range(lay.group):
        each = [lay.query_at(ref, h, start) for ref, start in queries]
        query = jnp.concatenate(each, axis=0)
        parts = [
            jnp.where(same, times_transposed(lay.kv_at(ref, 0, h, start), query), NEG)
            for ref, start in near
        ]
        parts += spatial_scores(lay, query, which, sources, h)
        exps, total, log = softmax_parts(parts, factor)
        result = spatial_values(lay, exps[nnear:], which, sources, h)
        for e, (ref, start) in zip(exps, near):
            result = result + transposed_times(lay.kv_at(ref, 1, h, start), e.astype(jnp.bfloat16))
        result = result / total
        spatial_logs.append(log)
        for r in range(nquery):
            mine = result[:, r * lay.nq : (r + 1) * lay.nq]
            other, log = temporal_part(lay, each[r], far[r], masks, h, factor)
            temporal_logs[r].append(log)
            if r:
                others[r - 1][lay.out(h), :] = mine.astype(jnp.bfloat16)
                others[r - 1][lay.out(h, lay.message), :] = other.astype(jnp.bfloat16)
            else:
                out_s[lay.out(h), :] = mine
                out_t[lay.out(h), :] = other
    for r in range(nquery):
        logs = [g[:, r * lay.nq : (r + 1) * lay.nq] for g in spatial_logs]
        if r:
            end = lay.group * HEAD_DIM
            others[r - 1][end : end + lay.logs, :] = split_rows(logs)
            others[r - 1][lay.message + end :, :] = split_rows(temporal_logs[r])
        else:
            out_l[...] = jnp.zeros(out_l.shape, jnp.float32)
            for h in range(lay.group):
                out_l[h : h + 1, :] = logs[h]
                out_l[lay.group + h : lay.group + h + 1, :] = temporal_logs[0][h]


def final_body(lay, across, mirrored, place_ref, *refs):
    own_s, own_t, own_l = refs[:3]
    others, refs = refs[3 : 2 + across], refs[2 + across :]
    out, refs = refs[-1], refs[:-1]
    end, size = lay.group * HEAD_DIM, lay.message
    for r in range(across):
        first = lax.rem(place_ref[0] + r, across) * lay.group
        kinds = []
        for kind in range(2):
            if r:
                values, start = others[r - 1], kind * size
                logs = joined_rows(values[start + end : start + size, :], lay.group)
            else:
                values, start = (own_s, own_t)[kind], 0
                at = kind * lay.group
                logs = [own_l[at + h : at + h + 1, :] for h in range(lay.group)]
            entries = [(values, start, logs)]
            if mirrored:
                values = refs[kind * across + r]
                entries.append((values, 0, joined_rows(values[end:, :], lay.group)))
            kinds.append(entries)
        for h in range(lay.group):
            total = None
            for entries in kinds:
                top = functools.reduce(jnp.maximum, [logs[h] for _, _, logs in entries])
                exps = [jnp.exp2((logs[h] - top) * LOG2E) for _, _, logs in entries]
                inverse = 1.0 / functools.reduce(jnp.add, exps)
                for e, (values, start, _) in zip(exps, entries):
                    term = values[lay.out(h, start), :].astype(jnp.float32) * (e * inverse)
                    total = term if total is None else total + term
            block = total.T.astype(jnp.bfloat16).reshape(out.shape[0], out.shape[1], HEAD_DIM)
            lanes = pl.ds(pl.multiple_of((first + h) * HEAD_DIM, HEAD_DIM), HEAD_DIM)
            out[:, :, lanes] = block


def moved(value, along, across, target, name=None):
    pairs = []
    for z in range(along):
        for x in range(across):
            to = target(z, x)
            pairs.append((z * across + x, to[0] * across + to[1]))
    return lax.ppermute(value, ("frames", "rows"), pairs)


def mirror_plan(tok_q, tok_kv, ref_kv, ref_ids, along, across):
    frames, rows, width = tok_q.shape
    nq, half, factor = frames * rows, along // 2, 1.0 / HEAD_DIM**0.5
    lay = Rows(width // HEAD_DIM // across, nq, ref_kv.shape[1], ref_kv.shape[2])
    f32, bf16 = jnp.float32, jnp.bfloat16
    call = Call(True)
    z, x = lax.axis_index("frames"), lax.axis_index("rows")
    total = along * frames

    def wrapped(gap):
        return (gap + total // 2) % total - total // 2

    base = z // half * half
    inner = [base + (z - base - s) % half for s in range(1, half)]
    offsets = [wrapped((z - (along - 1 - z)) * frames), 0] + [
        wrapped((other - z) * frames) for other in inner
    ]
    place = jnp.stack([jnp.asarray(v, jnp.int32) for v in (x, *offsets)])
    shapes = [((lay.query, HEAD_DIM), bf16), ((lay.kv, HEAD_DIM), bf16), ((lay.ref, HEAD_DIM), bf16)]
    shapes = shapes * across + [((lay.all, HEAD_DIM), bf16)] * (across - 1)
    packed = call(
        functools.partial(pack_body, lay, across, rows),
        shapes,
        place,
        ref_ids,
        tok_q,
        tok_kv,
        ref_kv,
        scalars=2,
    )
    qs, kvs, refs = (list(packed[i : 3 * across : 3]) for i in range(3))
    every = packed[3 * across :]

    def to_mirror(value, r):
        return moved(value, along, across, lambda z, x: (along - 1 - z, (x + r) % across))

    def to_half(value, s, r):
        return moved(
            value,
            along,
            across,
            lambda z, x: (z // half * half + (z % half + s) % half, (x + r) % across),
        )

    def to_side(value, r):
        return moved(value, along, across, lambda z, x: (z, (x + r) % across))

    mirrored = [to_mirror(qs[r], r) for r in range(across)]
    far_refs = [to_half(refs[r], s, r) for s in range(1, half) for r in range(across)]
    sides = [to_side(every[r - 1], r) for r in range(1, across)]
    far_kv = [[to_half(kvs[r], s, r) for r in range(across)] for s in range(1, half)]

    message = ((lay.message, HEAD_DIM), bf16)
    kv_blocks = [kvs[0], *sides]
    kv_starts = [0] + [lay.query] * (across - 1)
    partial_t = call(
        functools.partial(mirror_temporal_body, lay, rows, across, kv_starts, factor),
        [message] * across,
        place,
        *mirrored,
        *kv_blocks,
        scalars=1,
    )
    back_t = [to_mirror(partial_t[r], -r) for r in range(across)]
    sources = [refs[0], *sides, *far_refs]
    starts = [0] + [lay.query + lay.kv] * (across - 1) + [0] * len(far_refs)
    partial_s = call(
        functools.partial(mirror_spatial_body, lay, across, starts, factor),
        [message] * across,
        *mirrored,
        *sources,
    )
    back_s = [to_mirror(partial_s[r], -r) for r in range(across)]
    far = [[kv_blocks[r], *[block[r] for block in far_kv]] for r in range(across)]
    far_starts = [[kv_starts[r]] + [0] * len(far_kv) for r in range(across)]
    own = call(
        functools.partial(
            own_body,
            lay,
            rows,
            (across, len(sources), across, half),
            [0] * across + starts + kv_starts + sum(far_starts, []),
            factor,
        ),
        [
            ((lay.group * HEAD_DIM, nq), f32),
            ((lay.group * HEAD_DIM, nq), f32),
            ((round_up(2 * lay.group, 8), nq), f32),
        ]
        + [((2 * lay.message, HEAD_DIM), bf16)] * (across - 1),
        place,
        qs[0],
        *sides,
        *sources,
        *kv_blocks,
        *sum(far, []),
        scalars=1,
    )
    back = [to_side(own[3 + r - 1], -r) for r in range(1, across)]
    return call(
        functools.partial(final_body, lay, across, True),
        [(tok_q.shape, bf16)],
        place,
        *own[:3],
        *back,
        *back_s,
        *back_t,
        scalars=1,
        last=True,
    )[0]


def gathered_plan(tok_q, tok_kv, ref_kv, ref_ids, along, across):
    frames, rows, width = tok_q.shape
    nq, heads, factor = frames * rows, width // HEAD_DIM, 1.0 / HEAD_DIM**0.5
    f32, bf16 = jnp.float32, jnp.bfloat16
    call = Call(False)
    references = lax.all_gather(ref_kv, ("frames", "rows"), axis=2, tiled=True)
    lay = Rows(heads, nq, ref_kv.shape[1], references.shape[2])
    reach = (BAND - 1) // frames + 1
    assert 2 * reach + 1 <= along
    shifts = [s for r in range(1, reach + 1) for s in (r, -r)]
    place = jnp.asarray([0, 0, 0] + [-s * frames for s in shifts], jnp.int32)
    shapes = [((lay.query, HEAD_DIM), bf16), ((lay.kv, HEAD_DIM), bf16), ((lay.ref, HEAD_DIM), bf16)]
    qs, kvs, refs = call(
        functools.partial(pack_body, lay, 1, rows),
        shapes,
        place,
        ref_ids,
        tok_q,
        tok_kv,
        references,
        scalars=2,
    )
    sides = [
        moved(kvs, along, across, lambda z, x, r=r: (z, (x + r) % across)) for r in range(1, across)
    ]
    far = [moved(kvs, along, across, lambda z, x, s=s: ((z + s) % along, x)) for s in shifts]
    blocks = [qs, refs, kvs, *sides, kvs, *far]
    own = call(
        functools.partial(
            own_body,
            lay,
            rows,
            (1, 1, across, 1 + len(far)),
            [0] * len(blocks),
            factor,
        ),
        [
            ((heads * HEAD_DIM, nq), f32),
            ((heads * HEAD_DIM, nq), f32),
            ((round_up(2 * heads, 8), nq), f32),
        ],
        place,
        *blocks,
        scalars=1,
    )
    return call(
        functools.partial(final_body, lay, 1, False),
        [(tok_q.shape, bf16)],
        place,
        *own,
        scalars=1,
        last=True,
    )[0]


def local(tok_q, tok_kv, ref_kv, ref_ids):
    along, across = lax.axis_size("frames"), lax.axis_size("rows")
    frames, rows, width = tok_q.shape
    assert frames * rows == LANES
    apart = width // HEAD_DIM % across == 0 and ref_kv.shape[2] % TILE == 0
    near = along % 2 == 0 and frames >= BAND and along >= 4
    few = along // 2 * ref_kv.size <= 4 * tok_q.size * along
    plan = mirror_plan if apart and near and few else gathered_plan
    return plan(tok_q, tok_kv, ref_kv, ref_ids, along, across)


def solution(mesh):
    placed = (
        P(("clip", "frames"), "rows", "heads"),
        P(None, ("clip", "frames"), "rows", "heads"),
        P(None, "clip", ("frames", "rows"), "heads"),
        P(("clip", "frames")),
    )
    return jax.shard_map(
        local,
        mesh=mesh,
        in_specs=placed,
        out_specs=P(("clip", "frames"), "rows", "heads"),
        check_vma=False,
    )
```
